32 devices in a mesh: shard: 16 (over z, x, core), ctx: 2 (over y).
Axes of the slice: x: 2, y: 2, z: 4, core: 2. Of those that a mesh axis runs over, the one named last changes fastest.
Arguments:
- tokens: bfloat16 [8192, 576], P(('shard', 'ctx')), may hold values from -6 to 6
- cotangent: bfloat16 [8192, 576], P(('shard', 'ctx')), may hold values from -6 to 6
- seq_lengths: int32 [16], P('shard'), may hold values from 64 to 512, as said below
- attn_params: float32 [885888], P('shard')
- attn_first: float32 [885888], P('shard'), may hold values from -6 to 6
- attn_second: float32 [885888], P('shard'), may hold values from 1 to 100
- ffn_params: float32 [2654208], P('shard')
- ffn_first: float32 [2654208], P('shard'), may hold values from -6 to 6
- ffn_second: float32 [2654208], P('shard'), may hold values from 1 to 100
Outputs:
- outputs: bfloat16 [8192, 576], P(('shard', 'ctx'))
- grad_tokens: bfloat16 [8192, 576], P(('shard', 'ctx'))
- attn_grad: float32 [885888], P('shard')
- ffn_grad: float32 [2654208], P('shard')
- attn_new: float32 [885888], P('shard')
- attn_first_new: float32 [885888], P('shard')
- attn_second_new: float32 [885888], P('shard')
- ffn_new: float32 [2654208], P('shard')
- ffn_first_new: float32 [2654208], P('shard')
- ffn_second_new: float32 [2654208], P('shard')
The draws below stay inside these ranges and needn't reach their ends.
Inputs may be any that keep to these rules, and one draw needn't show every extreme that they name: `seq_lengths`: in every draw some sequence fills all 512 slots.
All inputs are finite; a program needn't handle non-finite values.
Results may differ from the reference program's by a relative error of at most 0.01.
The reference program's roundings to bfloat16 on the way count: a program that leaves them out, or rounds other values in their place, can miss the bound.
Values may be sent and summed in bfloat16 or wider, within the bound.
A program may use at most 128 MiB of HBM per device.

```python
import math
import jax
import jax.numpy as jnp
from jax import lax

MODEL_WIDTH = 576
QUERY_HEADS = 9
KEY_VALUE_HEADS = 3
HEAD_SIZE = 64
FF = 1536
TOK_DEV = 256
ADAM_STEP = 3
SEQ_SLOTS = 512
SEQS = 16
TOKENS = 8192
NA = 885888
NF = 2654208


def draw_seq_lengths(key, part):
    lengths = jax.random.randint(key, (SEQS,), TOK_DEV // 4, SEQ_SLOTS + 1)
    chosen = jax.random.randint(jax.random.fold_in(key, 7), (), 0, SEQS)
    return jnp.where(jnp.arange(SEQS) == chosen, SEQ_SLOTS, lengths).astype(jnp.int32)


def draw_sample(key, shape):
    return jnp.clip(jax.random.normal(key, shape, jnp.float32), -6.0, 6.0)


def draw_attn_params(key, part):
    sequence_lanes = jax.random.split(key, 6)
    w_query = draw_sample(sequence_lanes[0], (MODEL_WIDTH, QUERY_HEADS * HEAD_SIZE)) * MODEL_WIDTH ** (-0.5)
    key_matrix = draw_sample(sequence_lanes[1], (MODEL_WIDTH, KEY_VALUE_HEADS * HEAD_SIZE)) * MODEL_WIDTH ** (-0.5)
    value_matrix = draw_sample(sequence_lanes[2], (MODEL_WIDTH, KEY_VALUE_HEADS * HEAD_SIZE)) * MODEL_WIDTH ** (-0.5)
    w_out = draw_sample(sequence_lanes[3], (QUERY_HEADS * HEAD_SIZE, MODEL_WIDTH)) * (TOK_DEV / (QUERY_HEADS * HEAD_SIZE)) ** 0.5
    gain_one = 1.0 + 0.1 * jnp.clip(draw_sample(sequence_lanes[4], (MODEL_WIDTH,)), -3.0, 3.0)
    gain_two = 1.0 + 0.1 * jnp.clip(draw_sample(sequence_lanes[5], (MODEL_WIDTH,)), -3.0, 3.0)
    return jnp.concatenate([w_query.reshape(-1), key_matrix.reshape(-1), value_matrix.reshape(-1), w_out.reshape(-1), gain_one, gain_two]).astype(jnp.float32)


def draw_ffn_params(key, part):
    sequence_lanes = jax.random.split(key, 3)
    w_gate = draw_sample(sequence_lanes[0], (MODEL_WIDTH, FF)) * MODEL_WIDTH ** (-0.5)
    w_up = draw_sample(sequence_lanes[1], (MODEL_WIDTH, FF)) * MODEL_WIDTH ** (-0.5)
    w_down = draw_sample(sequence_lanes[2], (FF, MODEL_WIDTH)) * FF ** (-0.5)
    return jnp.concatenate([w_gate.reshape(-1), w_up.reshape(-1), w_down.reshape(-1)]).astype(jnp.float32)


def level_of(own_key, shape, shards, low, top_value):
    level, own = 1.0, jax.random.fold_in(own_key, 6)
    for dim, shards_of in shards:
        steps = jnp.exp(jax.random.uniform(jax.random.fold_in(own, dim), (shards_of,), jnp.float32, low / len(shards), top_value / len(shards)))
        level = level * jnp.repeat(steps, shape[dim] // shards_of).reshape([-1 if axis == dim else 1 for axis in range(len(shape))])
    return level


def centred(key, shape, deviation, bound, shards=(), dtype=jnp.bfloat16):
    values = deviation * jax.random.normal(key, shape, jnp.float32)
    if shards:
        values = values * level_of(key, shape, shards, -0.22, 0.18)
    return jnp.clip(values, -bound, bound).astype(dtype)


def setup_inputs(seed: int = 0) -> dict:
    arg_keys = jax.random.split(jax.random.key(seed), 10)
    return {
        "tokens": centred(arg_keys[0], (TOKENS, MODEL_WIDTH), 1.0, 6.0, ((0, 32),)),
        "cotangent": centred(arg_keys[1], (TOKENS, MODEL_WIDTH), 1.0, 6.0, ((0, 32),)),
        "seq_lengths": draw_seq_lengths(jax.random.fold_in(arg_keys[9], 71), 0),
        "attn_params": draw_attn_params(jax.random.fold_in(arg_keys[9], 71), 0),
        "attn_first": centred(arg_keys[4], (NA,), 1.0, 6.0, ((0, 16),), jnp.float32),
        "attn_second": jnp.clip(jnp.exp(math.log(100.0) - 4.6051702 * jax.random.uniform(arg_keys[5], (NA,), jnp.float32) ** level_of(arg_keys[5], (NA,), ((0, 16),), -0.2, 0.2)), 1.0, 100.0),
        "ffn_params": draw_ffn_params(jax.random.fold_in(arg_keys[9], 71), 0),
        "ffn_first": centred(arg_keys[7], (NF,), 1.0, 6.0, ((0, 16),), jnp.float32),
        "ffn_second": jnp.clip(jnp.exp(math.log(100.0) - 4.6051702 * jax.random.uniform(arg_keys[8], (NF,), jnp.float32) ** level_of(arg_keys[8], (NF,), ((0, 16),), -0.2, 0.2)), 1.0, 100.0),
    }


rms_eps = 1e-05
rope_base = 100000.0
beta_one = 0.9
beta_two = 0.95
learn_rate = 0.02
decay_rate = 0.1
adam_eps = 1e-08
masked_score = -1e+30

def split_flattened(flattened, shapes):
    pieces = []
    offset = 0
    for shape in shapes:
        width = 1
        for extent in shape:
            width = width * extent
        pieces.append(flattened[offset:offset + width].reshape(shape))
        offset = offset + width
    return pieces

def split_attention(flattened):
    return split_flattened(flattened, ((MODEL_WIDTH, QUERY_HEADS * HEAD_SIZE), (MODEL_WIDTH, KEY_VALUE_HEADS * HEAD_SIZE), (MODEL_WIDTH, KEY_VALUE_HEADS * HEAD_SIZE), (QUERY_HEADS * HEAD_SIZE, MODEL_WIDTH), (MODEL_WIDTH,), (MODEL_WIDTH,)))

def split_feedforward(flattened):
    return split_flattened(flattened, ((MODEL_WIDTH, FF), (MODEL_WIDTH, FF), (FF, MODEL_WIDTH)))

def rope_tables(positions):
    index = jnp.arange(HEAD_SIZE // 2).astype(jnp.float32)
    inverse = jnp.exp(index * (-2.0 * math.log(rope_base) / HEAD_SIZE))
    angles = positions.astype(jnp.float32)[:, None] * inverse[None, :]
    angles = jnp.concatenate([angles, angles], axis=1)
    return (jnp.cos(angles), jnp.sin(angles))

def apply_rotation(values, cosine_table, sine_table):
    half = values.shape[-1] // 2
    turned = jnp.concatenate([-values[..., half:], values[..., :half]], axis=-1)
    return values * cosine_table[:, None, :] + turned * sine_table[:, None, :]

def reverse_rotation(grads, cosine_table, sine_table):
    half = grads.shape[-1] // 2
    weighted = grads * sine_table[:, None, :]
    turned = jnp.concatenate([weighted[..., half:], -weighted[..., :half]], axis=-1)
    return grads * cosine_table[:, None, :] + turned

def norm_rows(values, gain):
    mean_sq = lax.optimization_barrier(jnp.mean(values * values, axis=-1, keepdims=True))
    inverse = lax.rsqrt(mean_sq + rms_eps)
    scaled = values * inverse
    return (scaled, inverse, (scaled * gain).astype(jnp.bfloat16))

def norm_back(grad_normed, scaled, inverse, gain):
    grad_scaled = grad_normed * gain
    grad_gain = lax.optimization_barrier(jnp.sum(grad_normed * scaled, axis=0))
    inner = lax.optimization_barrier(jnp.mean(grad_scaled * scaled, axis=-1, keepdims=True))
    return (inverse * (grad_scaled - scaled * inner), grad_gain)

def expand_heads(values):
    return lax.optimization_barrier(values).astype(jnp.float32)

def attend(query_rows, keys, values, mask):
    row_entries = query_rows.shape[0]
    scale = 1.0 / math.sqrt(HEAD_SIZE)
    grouped_heads = expand_heads(query_rows).reshape(row_entries, KEY_VALUE_HEADS, QUERY_HEADS // KEY_VALUE_HEADS, HEAD_SIZE)
    scores = jnp.einsum('tkgd,skd->kgts', grouped_heads, expand_heads(keys)) * scale
    scores = jnp.where(mask[None, None], scores, masked_score)
    top = lax.optimization_barrier(jnp.max(scores, axis=-1, keepdims=True))
    total = lax.optimization_barrier(jnp.sum(jnp.exp(scores - top), axis=-1, keepdims=True))
    log_total = top + jnp.log(total)
    probs = jnp.exp(scores - log_total).astype(jnp.bfloat16)
    mixture = jnp.einsum('kgts,skd->tkgd', expand_heads(probs), expand_heads(values))
    return (mixture.reshape(row_entries, QUERY_HEADS * HEAD_SIZE).astype(jnp.bfloat16), log_total)

def attend_back(query_rows, keys, values, mask, log_total, mixture, mixture_gradient):
    row_entries = query_rows.shape[0]
    scale = 1.0 / math.sqrt(HEAD_SIZE)
    grouped_heads = expand_heads(query_rows).reshape(row_entries, KEY_VALUE_HEADS, QUERY_HEADS // KEY_VALUE_HEADS, HEAD_SIZE)
    keys_wide = expand_heads(keys)
    values_wide = expand_heads(values)
    scores = jnp.einsum('tkgd,skd->kgts', grouped_heads, keys_wide) * scale
    scores = jnp.where(mask[None, None], scores, masked_score)
    probs = jnp.exp(scores - log_total)
    grouped_gradient = expand_heads(mixture_gradient).reshape(row_entries, KEY_VALUE_HEADS, QUERY_HEADS // KEY_VALUE_HEADS, HEAD_SIZE)
    grouped_mixture = expand_heads(mixture).reshape(row_entries, KEY_VALUE_HEADS, QUERY_HEADS // KEY_VALUE_HEADS, HEAD_SIZE)
    delta = jnp.einsum('tkgd,tkgd->kgt', grouped_gradient, grouped_mixture)
    grad_probs = jnp.einsum('tkgd,skd->kgts', grouped_gradient, values_wide)
    grad_scores = expand_heads((probs * (grad_probs - delta[..., None]) * scale).astype(jnp.bfloat16))
    grad_query = jnp.einsum('kgts,skd->tkgd', grad_scores, keys_wide).reshape(row_entries, QUERY_HEADS, HEAD_SIZE)
    key_gradient = jnp.einsum('kgts,tkgd->skd', grad_scores, grouped_heads)
    value_gradient = jnp.einsum('kgts,tkgd->skd', expand_heads(probs.astype(jnp.bfloat16)), grouped_gradient)
    return (grad_query, key_gradient, value_gradient)

def layer_rows(token_rows, cot_rows, length, attn_weights, ffn_weights):
    w_query, key_matrix, value_matrix, w_out, gain_one, gain_two = attn_weights
    w_gate, w_up, w_down = ffn_weights
    gain_one = gain_one.astype(jnp.float32)
    gain_two = gain_two.astype(jnp.float32)
    row_entries = token_rows.shape[0]
    positions = jnp.arange(row_entries).astype(jnp.int32)
    valid = (positions < length).astype(jnp.float32)[:, None]
    inputs = token_rows.astype(jnp.float32)
    scaled_one, inv_one, first_normed = norm_rows(inputs, gain_one)
    query_raw = jnp.dot(first_normed, w_query, preferred_element_type=jnp.float32).reshape(row_entries, QUERY_HEADS, HEAD_SIZE)
    unrotated_key = jnp.dot(first_normed, key_matrix, preferred_element_type=jnp.float32).reshape(row_entries, KEY_VALUE_HEADS, HEAD_SIZE)
    value_reduced = jnp.dot(first_normed, value_matrix, preferred_element_type=jnp.float32).astype(jnp.bfloat16).reshape(row_entries, KEY_VALUE_HEADS, HEAD_SIZE)
    cosine_table, sine_table = rope_tables(positions)
    query_low = apply_rotation(query_raw, cosine_table, sine_table).astype(jnp.bfloat16)
    key_reduced = apply_rotation(unrotated_key, cosine_table, sine_table).astype(jnp.bfloat16)
    mask = (positions[None, :] <= positions[:, None]) & (positions[None, :] < length)
    mixture, log_total = attend(query_low, key_reduced, value_reduced, mask)
    hidden = inputs + jnp.dot(mixture, w_out, preferred_element_type=jnp.float32)
    scaled_two, inv_two, normed_two = norm_rows(hidden, gain_two)
    gate = jnp.dot(normed_two, w_gate, preferred_element_type=jnp.float32)
    upward = jnp.dot(normed_two, w_up, preferred_element_type=jnp.float32)
    sigma = jax.nn.sigmoid(gate)
    activ = (gate * sigma * upward).astype(jnp.bfloat16)
    result = hidden + jnp.dot(activ, w_down, preferred_element_type=jnp.float32)
    outputs = (valid * result).astype(jnp.bfloat16)
    grad_result = valid * cot_rows.astype(jnp.float32)
    grad_low = grad_result.astype(jnp.bfloat16)
    grad_w_down = jnp.dot(activ.T, grad_low, preferred_element_type=jnp.float32)
    grad_activ = jnp.dot(grad_low, w_down.T, preferred_element_type=jnp.float32)
    grad_gate = (grad_activ * upward * sigma * (1.0 + gate * (1.0 - sigma))).astype(jnp.bfloat16)
    grad_upward = (grad_activ * gate * sigma).astype(jnp.bfloat16)
    grad_w_gate = jnp.dot(normed_two.T, grad_gate, preferred_element_type=jnp.float32)
    grad_w_up = jnp.dot(normed_two.T, grad_upward, preferred_element_type=jnp.float32)
    grad_normed_two = jnp.dot(grad_gate, w_gate.T, preferred_element_type=jnp.float32) + jnp.dot(grad_upward, w_up.T, preferred_element_type=jnp.float32)
    grad_hidden_part, grad_gain_two = norm_back(grad_normed_two, scaled_two, inv_two, gain_two)
    grad_hidden = grad_result + grad_hidden_part
    grad_hidden_low = grad_hidden.astype(jnp.bfloat16)
    grad_w_out = jnp.dot(mixture.T, grad_hidden_low, preferred_element_type=jnp.float32)
    mixture_gradient = jnp.dot(grad_hidden_low, w_out.T, preferred_element_type=jnp.float32).astype(jnp.bfloat16)
    grad_query, key_gradient, value_gradient = attend_back(query_low, key_reduced, value_reduced, mask, log_total, mixture, mixture_gradient)
    grad_query_raw = reverse_rotation(grad_query, cosine_table, sine_table).astype(jnp.bfloat16).reshape(row_entries, QUERY_HEADS * HEAD_SIZE)
    unrotated_key_gradient = reverse_rotation(key_gradient, cosine_table, sine_table).astype(jnp.bfloat16).reshape(row_entries, KEY_VALUE_HEADS * HEAD_SIZE)
    plain_value_gradient = value_gradient.astype(jnp.bfloat16).reshape(row_entries, KEY_VALUE_HEADS * HEAD_SIZE)
    grad_w_query = jnp.dot(first_normed.T, grad_query_raw, preferred_element_type=jnp.float32)
    grad_w_key = jnp.dot(first_normed.T, unrotated_key_gradient, preferred_element_type=jnp.float32)
    grad_w_value = jnp.dot(first_normed.T, plain_value_gradient, preferred_element_type=jnp.float32)
    grad_normed_one = jnp.dot(grad_query_raw, w_query.T, preferred_element_type=jnp.float32)
    grad_normed_one = grad_normed_one + jnp.dot(unrotated_key_gradient, key_matrix.T, preferred_element_type=jnp.float32)
    grad_normed_one = grad_normed_one + jnp.dot(plain_value_gradient, value_matrix.T, preferred_element_type=jnp.float32)
    grad_input_part, grad_gain_one = norm_back(grad_normed_one, scaled_one, inv_one, gain_one)
    grad_input = (grad_hidden + grad_input_part).astype(jnp.bfloat16)
    attn_term = jnp.concatenate([grad_w_query.reshape(-1), grad_w_key.reshape(-1), grad_w_value.reshape(-1), grad_w_out.reshape(-1), grad_gain_one, grad_gain_two])
    ffn_term = jnp.concatenate([grad_w_gate.reshape(-1), grad_w_up.reshape(-1), grad_w_down.reshape(-1)])
    return (outputs, grad_input, attn_term, ffn_term)

def adam_update(params, first, second, grads):
    first_new = beta_one * first + (1.0 - beta_one) * grads
    second_new = beta_two * second + (1.0 - beta_two) * grads * grads
    corr_one = 1.0 - beta_one ** ADAM_STEP
    corr_two = 1.0 - beta_two ** ADAM_STEP
    moved = first_new / corr_one / (jnp.sqrt(second_new / corr_two) + adam_eps)
    return (params - learn_rate * (moved + decay_rate * params), first_new, second_new)

def reference(tokens, cotangent, seq_lengths, attn_params, attn_first, attn_second, ffn_params, ffn_first, ffn_second):
    count = seq_lengths.shape[0]
    attn_weights = split_attention(attn_params.astype(jnp.bfloat16))
    ffn_weights = split_feedforward(ffn_params.astype(jnp.bfloat16))
    token_seqs = tokens.reshape(count, SEQ_SLOTS, MODEL_WIDTH)
    cot_seqs = cotangent.reshape(count, SEQ_SLOTS, MODEL_WIDTH)

    def one_sequence(carry, item):
        token_rows, cot_rows, length = item
        outputs, grad_input, attn_term, ffn_term = layer_rows(token_rows, cot_rows, length, attn_weights, ffn_weights)
        return ((carry[0] + attn_term, carry[1] + ffn_term), (outputs, grad_input))
    start = (jnp.zeros((attn_params.shape[0],), jnp.float32), jnp.zeros((ffn_params.shape[0],), jnp.float32))
    sums, stacked = lax.scan(one_sequence, start, (token_seqs, cot_seqs, seq_lengths))
    attn_grad, ffn_grad = sums
    outputs, grad_input = stacked
    attn_new, attn_first_new, attn_second_new = adam_update(attn_params, attn_first, attn_second, attn_grad)
    ffn_new, ffn_first_new, ffn_second_new = adam_update(ffn_params, ffn_first, ffn_second, ffn_grad)
    return (outputs.reshape(-1, MODEL_WIDTH), grad_input.reshape(-1, MODEL_WIDTH), attn_grad, ffn_grad, attn_new, attn_first_new, attn_second_new, ffn_new, ffn_first_new, ffn_second_new)
```

```python
import math

import jax
import jax.numpy as jnp
from jax import lax
from jax.sharding import PartitionSpec as P

MODEL_WIDTH = 576
QUERY_HEADS = 9
KEY_VALUE_HEADS = 3
HEAD_SIZE = 64
FF = 1536
ADAM_STEP = 3


rms_eps = 1e-05
rope_base = 100000.0
beta_one = 0.9
beta_two = 0.95
learn_rate = 0.02
decay_rate = 0.1
adam_eps = 1e-08
masked_score = -1e30


def split_flattened(flattened, shapes):
    pieces = []
    offset = 0
    for shape in shapes:
        width = 1
        for extent in shape:
            width = width * extent
        pieces.append(flattened[offset : offset + width].reshape(shape))
        offset = offset + width
    return pieces


def split_attention(flattened):
    return split_flattened(
        flattened,
        (
            (MODEL_WIDTH, QUERY_HEADS * HEAD_SIZE),
            (MODEL_WIDTH, KEY_VALUE_HEADS * HEAD_SIZE),
            (MODEL_WIDTH, KEY_VALUE_HEADS * HEAD_SIZE),
            (QUERY_HEADS * HEAD_SIZE, MODEL_WIDTH),
            (MODEL_WIDTH,),
            (MODEL_WIDTH,),
        ),
    )


def split_feedforward(flattened):
    return split_flattened(flattened, ((MODEL_WIDTH, FF), (MODEL_WIDTH, FF), (FF, MODEL_WIDTH)))


def rope_tables(positions):
    index = jnp.arange(HEAD_SIZE // 2).astype(jnp.float32)
    inverse = jnp.exp(index * (-2.0 * math.log(rope_base) / HEAD_SIZE))
    angles = positions.astype(jnp.float32)[:, None] * inverse[None, :]
    angles = jnp.concatenate([angles, angles], axis=1)
    return (jnp.cos(angles), jnp.sin(angles))


def apply_rotation(values, cosine_table, sine_table):
    half = values.shape[-1] // 2
    turned = jnp.concatenate([-values[..., half:], values[..., :half]], axis=-1)
    return values * cosine_table[:, None, :] + turned * sine_table[:, None, :]


def reverse_rotation(grads, cosine_table, sine_table):
    half = grads.shape[-1] // 2
    weighted = grads * sine_table[:, None, :]
    turned = jnp.concatenate([weighted[..., half:], -weighted[..., :half]], axis=-1)
    return grads * cosine_table[:, None, :] + turned


def norm_rows(values, gain):
    mean_sq = jnp.mean(values * values, axis=-1, keepdims=True)
    inverse = lax.rsqrt(mean_sq + rms_eps)
    scaled = values * inverse
    return (scaled, inverse, (scaled * gain).astype(jnp.bfloat16))


def norm_back(grad_normed, scaled, inverse, gain):
    grad_scaled = grad_normed * gain
    grad_gain = jnp.sum(grad_normed * scaled, axis=0)
    inner = jnp.mean(grad_scaled * scaled, axis=-1, keepdims=True)
    return (inverse * (grad_scaled - scaled * inner), grad_gain)


def attend(query_rows, keys, values, mask):
    row_entries = query_rows.shape[0]
    scale = 1.0 / math.sqrt(HEAD_SIZE)
    grouped_heads = query_rows.reshape(
        row_entries, KEY_VALUE_HEADS, QUERY_HEADS // KEY_VALUE_HEADS, HEAD_SIZE
    )
    scores = (
        jnp.einsum("tkgd,skd->kgts", grouped_heads, keys, preferred_element_type=jnp.float32)
        * scale
    )
    scores = jnp.where(mask[None, None], scores, masked_score)
    top = jnp.max(scores, axis=-1, keepdims=True)
    total = jnp.sum(jnp.exp(scores - top), axis=-1, keepdims=True)
    log_total = top + jnp.log(total)
    probs = jnp.exp(scores - log_total).astype(jnp.bfloat16)
    mixture = jnp.einsum("kgts,skd->tkgd", probs, values, preferred_element_type=jnp.float32)
    return (mixture.reshape(row_entries, QUERY_HEADS * HEAD_SIZE).astype(jnp.bfloat16), log_total)


def attend_back(query_rows, keys, values, mask, log_total, mixture, mixture_gradient):
    row_entries = query_rows.shape[0]
    head_group = QUERY_HEADS // KEY_VALUE_HEADS
    scale = 1.0 / math.sqrt(HEAD_SIZE)
    grouped_queries = query_rows.reshape(
        row_entries, KEY_VALUE_HEADS, head_group, HEAD_SIZE
    ).transpose(1, 0, 2, 3)
    gradient_groups = mixture_gradient.reshape(
        row_entries, KEY_VALUE_HEADS, head_group, HEAD_SIZE
    ).transpose(1, 0, 2, 3)
    mixture_groups = mixture.reshape(row_entries, KEY_VALUE_HEADS, head_group, HEAD_SIZE).transpose(
        1, 0, 2, 3
    )
    key_groups = keys.transpose(1, 0, 2)
    value_groups = values.transpose(1, 0, 2)

    def one_group(item):
        query_one, key_one, value_one, total_one, mixed_one, grad_one = item
        scores = (
            jnp.einsum("tgd,sd->gts", query_one, key_one, preferred_element_type=jnp.float32)
            * scale
        )
        scores = jnp.where(mask[None], scores, masked_score)
        probs = jnp.exp(scores - total_one)
        delta = jnp.einsum("tgd,tgd->gt", grad_one, mixed_one, preferred_element_type=jnp.float32)
        grad_probs = jnp.einsum(
            "tgd,sd->gts", grad_one, value_one, preferred_element_type=jnp.float32
        )
        grad_scores = (probs * (grad_probs - delta[..., None]) * scale).astype(jnp.bfloat16)
        grad_query = jnp.einsum(
            "gts,sd->tgd", grad_scores, key_one, preferred_element_type=jnp.float32
        )
        key_gradient = jnp.einsum(
            "gts,tgd->sd", grad_scores, query_one, preferred_element_type=jnp.float32
        )
        value_gradient = jnp.einsum(
            "gts,tgd->sd", probs.astype(jnp.bfloat16), grad_one, preferred_element_type=jnp.float32
        )
        return (grad_query, key_gradient, value_gradient)

    grad_query, key_gradient, value_gradient = lax.map(
        one_group,
        (grouped_queries, key_groups, value_groups, log_total, mixture_groups, gradient_groups),
    )
    grad_query = grad_query.transpose(1, 0, 2, 3).reshape(row_entries, QUERY_HEADS, HEAD_SIZE)
    return (grad_query, key_gradient.transpose(1, 0, 2), value_gradient.transpose(1, 0, 2))


def adam_update(params, first, second, grads):
    first_new = beta_one * first + (1.0 - beta_one) * grads
    second_new = beta_two * second + (1.0 - beta_two) * grads * grads
    corr_one = 1.0 - beta_one**ADAM_STEP
    corr_two = 1.0 - beta_two**ADAM_STEP
    moved = first_new / corr_one / (jnp.sqrt(second_new / corr_two) + adam_eps)
    return (params - learn_rate * (moved + decay_rate * params), first_new, second_new)


LANES = 128


def swap_pairs(count, distance):
    return [(index, index ^ distance) for index in range(count)]


def halve_stage(table, bits, bit, owners, index):
    axis = bits.index(bit)
    mine = (index >> bit) & 1
    send = lax.dynamic_index_in_dim(table, 1 - mine, axis, keepdims=False)
    keep = lax.dynamic_index_in_dim(table, mine, axis, keepdims=False)
    got = lax.ppermute(send, "shard", swap_pairs(owners, 1 << bit))
    total = (keep.astype(jnp.float32) + got.astype(jnp.float32)).astype(jnp.bfloat16)
    return total, [b for b in bits if b != bit]


def scatter_sum(table, owners, order):
    index = lax.axis_index("shard")
    count = owners.bit_length() - 1
    bits = list(range(count))[::-1]
    table = table.reshape((2,) * count + table.shape[1:])
    for bit in order:
        table, bits = halve_stage(table, bits, bit, owners, index)
    other = lax.ppermute(table, "ctx", swap_pairs(2, 1))
    return table.astype(jnp.float32) + other.astype(jnp.float32)


def scatter_parts(table, owners):
    count = owners.bit_length() - 1
    low = list(range(count))
    orders = ([0] + low[1:], [0] + low[2:][::-1] + [1])
    rows = table.shape[1]
    cut = rows // 2 // 16 * 16
    one = scatter_sum(table[:, :cut], owners, orders[0])
    two = scatter_sum(table[:, cut:], owners, orders[1])
    return jnp.concatenate([one, two], axis=0).reshape(-1)


def body(
    tokens,
    cotangent,
    seq_lengths,
    attn_params,
    attn_first,
    attn_second,
    ffn_params,
    ffn_first,
    ffn_second,
):
    row_entries = tokens.shape[0]
    ctx_count = lax.axis_size("ctx")
    ctx_index = lax.axis_index("ctx")
    owners = lax.axis_size("shard")
    slot_entries = row_entries * ctx_count
    length = seq_lengths[0]
    attn_columns = attn_params.shape[0]
    attn_rows = -(-attn_columns // (16 * LANES)) * 16
    attn_pad = attn_rows * LANES - attn_columns
    attn_low = jnp.pad(attn_params.astype(jnp.bfloat16), (0, attn_pad))
    attn_whole = lax.all_gather(attn_low, "shard", axis=0, tiled=True)
    attn_whole = attn_whole.reshape(owners, attn_rows * LANES)[:, :attn_columns].reshape(-1)
    ffn_whole = lax.all_gather(ffn_params.astype(jnp.bfloat16), "shard", axis=0, tiled=True)
    w_query, key_matrix, value_matrix, w_out, gain_one, gain_two = split_attention(attn_whole)
    w_gate, w_up, w_down = split_feedforward(ffn_whole)
    gain_one = gain_one.astype(jnp.float32)
    gain_two = gain_two.astype(jnp.float32)
    positions = ctx_index * row_entries + jnp.arange(row_entries)
    key_positions = jnp.arange(slot_entries)
    valid = (positions < length).astype(jnp.float32)[:, None]
    has_rows = ctx_index * row_entries < length
    mask = (key_positions[None, :] <= positions[:, None]) & (key_positions[None, :] < length)
    inputs = tokens.astype(jnp.float32)
    scaled_one, inv_one, first_normed = norm_rows(inputs, gain_one)
    query_raw = jnp.dot(first_normed, w_query, preferred_element_type=jnp.float32).reshape(
        row_entries, QUERY_HEADS, HEAD_SIZE
    )
    unrotated_key = jnp.dot(first_normed, key_matrix, preferred_element_type=jnp.float32).reshape(
        row_entries, KEY_VALUE_HEADS, HEAD_SIZE
    )
    value_reduced = jnp.dot(first_normed, value_matrix, preferred_element_type=jnp.float32).astype(
        jnp.bfloat16
    )
    cosine_table, sine_table = rope_tables(positions)
    query_low = apply_rotation(query_raw, cosine_table, sine_table).astype(jnp.bfloat16)
    key_reduced = (
        apply_rotation(unrotated_key, cosine_table, sine_table)
        .astype(jnp.bfloat16)
        .reshape(row_entries, KEY_VALUE_HEADS * HEAD_SIZE)
    )
    key_columns = KEY_VALUE_HEADS * HEAD_SIZE
    both = jnp.concatenate([key_reduced, value_reduced], axis=1)
    other_both = lax.ppermute(both, "ctx", swap_pairs(2, 1))
    first = ctx_index == 0
    full_both = jnp.concatenate(
        [jnp.where(first, both, other_both), jnp.where(first, other_both, both)], axis=0
    )
    full_keys = full_both[:, :key_columns]
    full_values = full_both[:, key_columns:]
    full_keys = full_keys.reshape(slot_entries, KEY_VALUE_HEADS, HEAD_SIZE)
    full_values = full_values.reshape(slot_entries, KEY_VALUE_HEADS, HEAD_SIZE)
    mixture, log_total = lax.cond(
        has_rows,
        lambda: attend(query_low, full_keys, full_values, mask),
        lambda: (
            jnp.zeros((row_entries, QUERY_HEADS * HEAD_SIZE), jnp.bfloat16),
            jnp.zeros(
                (KEY_VALUE_HEADS, QUERY_HEADS // KEY_VALUE_HEADS, row_entries, 1), jnp.float32
            ),
        ),
    )
    hidden = inputs + jnp.dot(mixture, w_out, preferred_element_type=jnp.float32)
    scaled_two, inv_two, normed_two = norm_rows(hidden, gain_two)
    gate = jnp.dot(normed_two, w_gate, preferred_element_type=jnp.float32)
    upward = jnp.dot(normed_two, w_up, preferred_element_type=jnp.float32)
    sigma = jax.nn.sigmoid(gate)
    activ = (gate * sigma * upward).astype(jnp.bfloat16)
    result = hidden + jnp.dot(activ, w_down, preferred_element_type=jnp.float32)
    outputs = (valid * result).astype(jnp.bfloat16)
    grad_result = valid * cotangent.astype(jnp.float32)
    grad_low = grad_result.astype(jnp.bfloat16)
    grad_w_down = jnp.dot(activ.T, grad_low, preferred_element_type=jnp.float32)
    grad_activ = jnp.dot(grad_low, w_down.T, preferred_element_type=jnp.float32)
    grad_gate = (grad_activ * upward * sigma * (1.0 + gate * (1.0 - sigma))).astype(jnp.bfloat16)
    grad_upward = (grad_activ * gate * sigma).astype(jnp.bfloat16)
    grad_w_gate = jnp.dot(normed_two.T, grad_gate, preferred_element_type=jnp.float32)
    grad_w_up = jnp.dot(normed_two.T, grad_upward, preferred_element_type=jnp.float32)
    low = jnp.bfloat16
    ffn_term = jnp.concatenate(
        [
            grad_w_gate.astype(low).reshape(-1),
            grad_w_up.astype(low).reshape(-1),
            grad_w_down.astype(low).reshape(-1),
        ]
    )
    ffn_joined = scatter_parts(ffn_term.reshape(owners, -1, LANES), owners)
    grad_normed_two = jnp.dot(grad_gate, w_gate.T, preferred_element_type=jnp.float32) + jnp.dot(
        grad_upward, w_up.T, preferred_element_type=jnp.float32
    )
    grad_hidden_part, grad_gain_two = norm_back(grad_normed_two, scaled_two, inv_two, gain_two)
    grad_hidden = grad_result + grad_hidden_part
    grad_hidden_low = grad_hidden.astype(jnp.bfloat16)
    grad_w_out = jnp.dot(mixture.T, grad_hidden_low, preferred_element_type=jnp.float32)
    mixture_gradient = jnp.dot(grad_hidden_low, w_out.T, preferred_element_type=jnp.float32).astype(
        jnp.bfloat16
    )
    grad_query, full_key_gradient, full_value_gradient = lax.cond(
        has_rows,
        lambda: attend_back(
            query_low, full_keys, full_values, mask, log_total, mixture, mixture_gradient
        ),
        lambda: (
            jnp.zeros((row_entries, QUERY_HEADS, HEAD_SIZE), jnp.float32),
            jnp.zeros((slot_entries, KEY_VALUE_HEADS, HEAD_SIZE), jnp.float32),
            jnp.zeros((slot_entries, KEY_VALUE_HEADS, HEAD_SIZE), jnp.float32),
        ),
    )
    full_gradient = jnp.concatenate(
        [
            full_key_gradient.reshape(slot_entries, key_columns),
            full_value_gradient.reshape(slot_entries, key_columns),
        ],
        axis=1,
    )
    halves = full_gradient.reshape(2, row_entries, 2 * key_columns)
    away = lax.dynamic_index_in_dim(halves, 1 - ctx_index, 0, keepdims=False)
    home = lax.dynamic_index_in_dim(halves, ctx_index, 0, keepdims=False)
    got = lax.ppermute(away.astype(jnp.bfloat16), "ctx", swap_pairs(2, 1))
    summed = home + got.astype(jnp.float32)
    key_gradient = summed[:, :key_columns]
    value_gradient = summed[:, key_columns:]
    grad_query_raw = (
        reverse_rotation(grad_query, cosine_table, sine_table)
        .astype(jnp.bfloat16)
        .reshape(row_entries, QUERY_HEADS * HEAD_SIZE)
    )
    unrotated_key_gradient = (
        reverse_rotation(
            key_gradient.reshape(row_entries, KEY_VALUE_HEADS, HEAD_SIZE), cosine_table, sine_table
        )
        .astype(jnp.bfloat16)
        .reshape(row_entries, KEY_VALUE_HEADS * HEAD_SIZE)
    )
    plain_value_gradient = value_gradient.astype(jnp.bfloat16)
    grad_w_query = jnp.dot(first_normed.T, grad_query_raw, preferred_element_type=jnp.float32)
    grad_w_key = jnp.dot(first_normed.T, unrotated_key_gradient, preferred_element_type=jnp.float32)
    grad_w_value = jnp.dot(first_normed.T, plain_value_gradient, preferred_element_type=jnp.float32)
    grad_normed_one = jnp.dot(grad_query_raw, w_query.T, preferred_element_type=jnp.float32)
    grad_normed_one = grad_normed_one + jnp.dot(
        unrotated_key_gradient, key_matrix.T, preferred_element_type=jnp.float32
    )
    grad_normed_one = grad_normed_one + jnp.dot(
        plain_value_gradient, value_matrix.T, preferred_element_type=jnp.float32
    )
    grad_input_part, grad_gain_one = norm_back(grad_normed_one, scaled_one, inv_one, gain_one)
    grad_tokens = (grad_hidden + grad_input_part).astype(jnp.bfloat16)
    attn_term = jnp.concatenate(
        [
            grad_w_query.astype(low).reshape(-1),
            grad_w_key.astype(low).reshape(-1),
            grad_w_value.astype(low).reshape(-1),
            grad_w_out.astype(low).reshape(-1),
            grad_gain_one.astype(low),
            grad_gain_two.astype(low),
        ]
    )
    attn_table = jnp.pad(attn_term.reshape(owners, attn_columns), ((0, 0), (0, attn_pad)))
    attn_grad = scatter_parts(attn_table.reshape(owners, attn_rows, LANES), owners)[:attn_columns]
    attn_new, attn_first_new, attn_second_new = adam_update(
        attn_params, attn_first, attn_second, attn_grad
    )
    ffn_new, ffn_first_new, ffn_second_new = adam_update(
        ffn_params, ffn_first, ffn_second, ffn_joined
    )
    return (
        outputs,
        grad_tokens,
        attn_grad,
        ffn_joined,
        attn_new,
        attn_first_new,
        attn_second_new,
        ffn_new,
        ffn_first_new,
        ffn_second_new,
    )


def solution(mesh):
    return jax.shard_map(
        body,
        mesh=mesh,
        in_specs=(
            P(("shard", "ctx"), None),
            P(("shard", "ctx"), None),
            P("shard"),
            P("shard"),
            P("shard"),
            P("shard"),
            P("shard"),
            P("shard"),
            P("shard"),
        ),
        out_specs=(
            P(("shard", "ctx"), None),
            P(("shard", "ctx"), None),
            P("shard"),
            P("shard"),
            P("shard"),
            P("shard"),
            P("shard"),
            P("shard"),
            P("shard"),
            P("shard"),
        ),
        check_vma=False,
    )
```

```python
import math

import jax
import jax.numpy as jnp
from jax import lax
from jax.sharding import PartitionSpec as P

MODEL_WIDTH = 576
QUERY_HEADS = 9
KEY_VALUE_HEADS = 3
HEAD_SIZE = 64
FF = 1536
ADAM_STEP = 3


rms_eps = 1e-05
rope_base = 100000.0
beta_one = 0.9
beta_two = 0.95
learn_rate = 0.02
decay_rate = 0.1
adam_eps = 1e-08
masked_score = -1e30


def split_flattened(flattened, shapes):
    pieces = []
    offset = 0
    for shape in shapes:
        width = 1
        for extent in shape:
            width = width * extent
        pieces.append(flattened[offset : offset + width].reshape(shape))
        offset = offset + width
    return pieces


def split_attention(flattened):
    return split_flattened(
        flattened,
        (
            (MODEL_WIDTH, QUERY_HEADS * HEAD_SIZE),
            (MODEL_WIDTH, KEY_VALUE_HEADS * HEAD_SIZE),
            (MODEL_WIDTH, KEY_VALUE_HEADS * HEAD_SIZE),
            (QUERY_HEADS * HEAD_SIZE, MODEL_WIDTH),
            (MODEL_WIDTH,),
            (MODEL_WIDTH,),
        ),
    )


def split_feedforward(flattened):
    return split_flattened(flattened, ((MODEL_WIDTH, FF), (MODEL_WIDTH, FF), (FF, MODEL_WIDTH)))


def rope_tables(positions):
    index = jnp.arange(HEAD_SIZE // 2).astype(jnp.float32)
    inverse = jnp.exp(index * (-2.0 * math.log(rope_base) / HEAD_SIZE))
    angles = positions.astype(jnp.float32)[:, None] * inverse[None, :]
    angles = jnp.concatenate([angles, angles], axis=1)
    return (jnp.cos(angles), jnp.sin(angles))


def apply_rotation(values, cosine_table, sine_table):
    half = values.shape[-1] // 2
    turned = jnp.concatenate([-values[..., half:], values[..., :half]], axis=-1)
    return values * cosine_table[:, None, :] + turned * sine_table[:, None, :]


def reverse_rotation(grads, cosine_table, sine_table):
    half = grads.shape[-1] // 2
    weighted = grads * sine_table[:, None, :]
    turned = jnp.concatenate([weighted[..., half:], -weighted[..., :half]], axis=-1)
    return grads * cosine_table[:, None, :] + turned


def norm_rows(values, gain):
    mean_sq = jnp.mean(values * values, axis=-1, keepdims=True)
    inverse = lax.rsqrt(mean_sq + rms_eps)
    scaled = values * inverse
    return (scaled, inverse, (scaled * gain).astype(jnp.bfloat16))


def norm_back(grad_normed, scaled, inverse, gain):
    grad_scaled = grad_normed * gain
    grad_gain = jnp.sum(grad_normed * scaled, axis=0)
    inner = jnp.mean(grad_scaled * scaled, axis=-1, keepdims=True)
    return (inverse * (grad_scaled - scaled * inner), grad_gain)


def attend(query_rows, keys, values, mask):
    row_entries = query_rows.shape[0]
    scale = 1.0 / math.sqrt(HEAD_SIZE)
    grouped_heads = query_rows.reshape(
        row_entries, KEY_VALUE_HEADS, QUERY_HEADS // KEY_VALUE_HEADS, HEAD_SIZE
    )
    scores = (
        jnp.einsum("tkgd,skd->kgts", grouped_heads, keys, preferred_element_type=jnp.float32)
        * scale
    )
    scores = jnp.where(mask[None, None], scores, masked_score)
    top = jnp.max(scores, axis=-1, keepdims=True)
    total = jnp.sum(jnp.exp(scores - top), axis=-1, keepdims=True)
    log_total = top + jnp.log(total)
    probs = jnp.exp(scores - log_total).astype(jnp.bfloat16)
    mixture = jnp.einsum("kgts,skd->tkgd", probs, values, preferred_element_type=jnp.float32)
    return (mixture.reshape(row_entries, QUERY_HEADS * HEAD_SIZE).astype(jnp.bfloat16), log_total)


def attend_back(
    query_rows, keys, values, mask, log_total, mixture, mixture_gradient, parts, owners, index
):
    row_entries = query_rows.shape[0]
    head_group = QUERY_HEADS // KEY_VALUE_HEADS
    scale = 1.0 / math.sqrt(HEAD_SIZE)
    grouped_queries = query_rows.reshape(
        row_entries, KEY_VALUE_HEADS, head_group, HEAD_SIZE
    ).transpose(1, 0, 2, 3)
    gradient_groups = mixture_gradient.reshape(
        row_entries, KEY_VALUE_HEADS, head_group, HEAD_SIZE
    ).transpose(1, 0, 2, 3)
    mixture_groups = mixture.reshape(row_entries, KEY_VALUE_HEADS, head_group, HEAD_SIZE).transpose(
        1, 0, 2, 3
    )
    key_groups = keys.transpose(1, 0, 2)
    value_groups = values.transpose(1, 0, 2)

    def one_group(item):
        query_one, key_one, value_one, total_one, mixed_one, grad_one = item
        scores = (
            jnp.einsum("tgd,sd->gts", query_one, key_one, preferred_element_type=jnp.float32)
            * scale
        )
        scores = jnp.where(mask[None], scores, masked_score)
        probs = jnp.exp(scores - total_one)
        delta = jnp.einsum("tgd,tgd->gt", grad_one, mixed_one, preferred_element_type=jnp.float32)
        grad_probs = jnp.einsum(
            "tgd,sd->gts", grad_one, value_one, preferred_element_type=jnp.float32
        )
        grad_scores = (probs * (grad_probs - delta[..., None]) * scale).astype(jnp.bfloat16)
        grad_query = jnp.einsum(
            "gts,sd->tgd", grad_scores, key_one, preferred_element_type=jnp.float32
        )
        key_gradient = jnp.einsum(
            "gts,tgd->sd", grad_scores, query_one, preferred_element_type=jnp.float32
        )
        value_gradient = jnp.einsum(
            "gts,tgd->sd", probs.astype(jnp.bfloat16), grad_one, preferred_element_type=jnp.float32
        )
        return (grad_query, key_gradient, value_gradient)

    results = []
    steps = owners.bit_length() - 1
    for group in range(KEY_VALUE_HEADS):
        grad_one = gradient_groups[group]
        if group > 0 and group <= steps:
            parts = step_parts(parts, group - 1, owners, index)
            parts, (grad_one, _) = tie(parts, (grad_one, results[-1][0]))
        results.append(
            one_group(
                (
                    grouped_queries[group],
                    key_groups[group],
                    value_groups[group],
                    log_total[group],
                    mixture_groups[group],
                    grad_one,
                )
            )
        )
    if KEY_VALUE_HEADS <= steps:
        parts = step_parts(parts, KEY_VALUE_HEADS - 1, owners, index)
    grad_query, key_gradient, value_gradient = [jnp.stack(item) for item in zip(*results)]
    grad_query = grad_query.transpose(1, 0, 2, 3).reshape(row_entries, QUERY_HEADS, HEAD_SIZE)
    return (grad_query, key_gradient.transpose(1, 0, 2), value_gradient.transpose(1, 0, 2), parts)


def adam_update(params, first, second, grads):
    first_new = beta_one * first + (1.0 - beta_one) * grads
    second_new = beta_two * second + (1.0 - beta_two) * grads * grads
    corr_one = 1.0 - beta_one**ADAM_STEP
    corr_two = 1.0 - beta_two**ADAM_STEP
    moved = first_new / corr_one / (jnp.sqrt(second_new / corr_two) + adam_eps)
    return (params - learn_rate * (moved + decay_rate * params), first_new, second_new)


LANES = 128


def swap_pairs(count, distance):
    return [(index, index ^ distance) for index in range(count)]


def halve_stage(table, bits, bit, owners, index):
    axis = bits.index(bit)
    mine = (index >> bit) & 1
    send = lax.dynamic_index_in_dim(table, 1 - mine, axis, keepdims=False)
    keep = lax.dynamic_index_in_dim(table, mine, axis, keepdims=False)
    got = lax.ppermute(send, "shard", swap_pairs(owners, 1 << bit))
    total = (keep.astype(jnp.float32) + got.astype(jnp.float32)).astype(jnp.bfloat16)
    return total, [b for b in bits if b != bit]


def bit_orders(owners):
    low = list(range(owners.bit_length() - 1))
    return ([0] + low[1:], [0] + low[2:][::-1] + [1])


def open_parts(table, owners):
    count = owners.bit_length() - 1
    cut = table.shape[1] // 32 * 16
    pieces = (table[:, :cut], table[:, cut:])
    return [
        (piece.reshape((2,) * count + piece.shape[1:]), list(range(count))[::-1])
        for piece in pieces
    ]


def step_parts(parts, step, owners, index):
    return [
        halve_stage(table, bits, order[step], owners, index)
        for (table, bits), order in zip(parts, bit_orders(owners))
    ]


def tie(parts, other):
    tables, other = lax.optimization_barrier(([table for table, _ in parts], other))
    return [(table, bits) for table, (_, bits) in zip(tables, parts)], other


def close_parts(parts):
    sums = []
    for table, _ in parts:
        got = lax.ppermute(table, "ctx", swap_pairs(2, 1))
        sums.append(table.astype(jnp.float32) + got.astype(jnp.float32))
    return jnp.concatenate(sums, axis=0).reshape(-1)


def doubling_gather(share, owners, index):
    count = owners.bit_length() - 1
    table = share
    for place, bit in enumerate(range(count)[::-1]):
        got = lax.ppermute(table, "shard", swap_pairs(owners, 1 << bit))
        low_first = ((index >> bit) & 1) == 0
        table = jnp.stack(
            [jnp.where(low_first, table, got), jnp.where(low_first, got, table)], axis=place
        )
    return table.reshape((owners,) + share.shape)


def body(
    tokens,
    cotangent,
    seq_lengths,
    attn_params,
    attn_first,
    attn_second,
    ffn_params,
    ffn_first,
    ffn_second,
):
    row_entries = tokens.shape[0]
    ctx_count = lax.axis_size("ctx")
    ctx_index = lax.axis_index("ctx")
    owners = lax.axis_size("shard")
    slot_entries = row_entries * ctx_count
    length = seq_lengths[0]
    attn_columns = attn_params.shape[0]
    attn_rows = -(-attn_columns // (16 * LANES)) * 16
    attn_pad = attn_rows * LANES - attn_columns
    attn_low = jnp.pad(attn_params.astype(jnp.bfloat16), (0, attn_pad))
    shard_index = lax.axis_index("shard")
    attn_whole = doubling_gather(attn_low.reshape(attn_rows, LANES), owners, shard_index)
    attn_whole = attn_whole.reshape(owners, attn_rows * LANES)[:, :attn_columns].reshape(-1)
    ffn_whole = lax.all_gather(ffn_params.astype(jnp.bfloat16), "shard", axis=0, tiled=True)
    w_query, key_matrix, value_matrix, w_out, gain_one, gain_two = split_attention(attn_whole)
    w_gate, w_up, w_down = split_feedforward(ffn_whole)
    gain_one = gain_one.astype(jnp.float32)
    gain_two = gain_two.astype(jnp.float32)
    positions = ctx_index * row_entries + jnp.arange(row_entries)
    key_positions = jnp.arange(slot_entries)
    valid = (positions < length).astype(jnp.float32)[:, None]
    mask = (key_positions[None, :] <= positions[:, None]) & (key_positions[None, :] < length)
    inputs = tokens.astype(jnp.float32)
    scaled_one, inv_one, first_normed = norm_rows(inputs, gain_one)
    query_raw = jnp.dot(first_normed, w_query, preferred_element_type=jnp.float32).reshape(
        row_entries, QUERY_HEADS, HEAD_SIZE
    )
    unrotated_key = jnp.dot(first_normed, key_matrix, preferred_element_type=jnp.float32).reshape(
        row_entries, KEY_VALUE_HEADS, HEAD_SIZE
    )
    value_reduced = jnp.dot(first_normed, value_matrix, preferred_element_type=jnp.float32).astype(
        jnp.bfloat16
    )
    cosine_table, sine_table = rope_tables(positions)
    query_low = apply_rotation(query_raw, cosine_table, sine_table).astype(jnp.bfloat16)
    key_reduced = (
        apply_rotation(unrotated_key, cosine_table, sine_table)
        .astype(jnp.bfloat16)
        .reshape(row_entries, KEY_VALUE_HEADS * HEAD_SIZE)
    )
    key_columns = KEY_VALUE_HEADS * HEAD_SIZE
    both = jnp.concatenate([key_reduced, value_reduced], axis=1)
    other_both = lax.ppermute(both, "ctx", swap_pairs(2, 1))
    first = ctx_index == 0
    full_both = jnp.concatenate(
        [jnp.where(first, both, other_both), jnp.where(first, other_both, both)], axis=0
    )
    full_keys = full_both[:, :key_columns]
    full_values = full_both[:, key_columns:]
    full_keys = full_keys.reshape(slot_entries, KEY_VALUE_HEADS, HEAD_SIZE)
    full_values = full_values.reshape(slot_entries, KEY_VALUE_HEADS, HEAD_SIZE)
    mixture, log_total = attend(query_low, full_keys, full_values, mask)
    hidden = inputs + jnp.dot(mixture, w_out, preferred_element_type=jnp.float32)
    scaled_two, inv_two, normed_two = norm_rows(hidden, gain_two)
    gate = jnp.dot(normed_two, w_gate, preferred_element_type=jnp.float32)
    upward = jnp.dot(normed_two, w_up, preferred_element_type=jnp.float32)
    sigma = jax.nn.sigmoid(gate)
    activ = (gate * sigma * upward).astype(jnp.bfloat16)
    result = hidden + jnp.dot(activ, w_down, preferred_element_type=jnp.float32)
    outputs = (valid * result).astype(jnp.bfloat16)
    grad_result = valid * cotangent.astype(jnp.float32)
    grad_low = grad_result.astype(jnp.bfloat16)
    grad_w_down = jnp.dot(activ.T, grad_low, preferred_element_type=jnp.float32)
    grad_activ = jnp.dot(grad_low, w_down.T, preferred_element_type=jnp.float32)
    grad_gate = (grad_activ * upward * sigma * (1.0 + gate * (1.0 - sigma))).astype(jnp.bfloat16)
    grad_upward = (grad_activ * gate * sigma).astype(jnp.bfloat16)
    grad_w_gate = jnp.dot(normed_two.T, grad_gate, preferred_element_type=jnp.float32)
    grad_w_up = jnp.dot(normed_two.T, grad_upward, preferred_element_type=jnp.float32)
    low = jnp.bfloat16
    ffn_term = jnp.concatenate(
        [
            grad_w_gate.astype(low).reshape(-1),
            grad_w_up.astype(low).reshape(-1),
            grad_w_down.astype(low).reshape(-1),
        ]
    )
    ffn_parts = open_parts(ffn_term.reshape(owners, -1, LANES), owners)
    grad_normed_two = jnp.dot(grad_gate, w_gate.T, preferred_element_type=jnp.float32) + jnp.dot(
        grad_upward, w_up.T, preferred_element_type=jnp.float32
    )
    grad_hidden_part, grad_gain_two = norm_back(grad_normed_two, scaled_two, inv_two, gain_two)
    grad_hidden = grad_result + grad_hidden_part
    grad_hidden_low = grad_hidden.astype(jnp.bfloat16)
    grad_w_out = jnp.dot(mixture.T, grad_hidden_low, preferred_element_type=jnp.float32)
    mixture_gradient = jnp.dot(grad_hidden_low, w_out.T, preferred_element_type=jnp.float32).astype(
        jnp.bfloat16
    )
    steps = owners.bit_length() - 1
    grad_query, full_key_gradient, full_value_gradient, ffn_parts = attend_back(
        query_low,
        full_keys,
        full_values,
        mask,
        log_total,
        mixture,
        mixture_gradient,
        ffn_parts,
        owners,
        shard_index,
    )
    for step in range(KEY_VALUE_HEADS, steps):
        ffn_parts = step_parts(ffn_parts, step, owners, shard_index)
    ffn_joined = close_parts(ffn_parts)
    full_gradient = jnp.concatenate(
        [
            full_key_gradient.reshape(slot_entries, key_columns),
            full_value_gradient.reshape(slot_entries, key_columns),
        ],
        axis=1,
    )
    halves = full_gradient.reshape(2, row_entries, 2 * key_columns)
    away = lax.dynamic_index_in_dim(halves, 1 - ctx_index, 0, keepdims=False)
    home = lax.dynamic_index_in_dim(halves, ctx_index, 0, keepdims=False)
    got = lax.ppermute(away.astype(jnp.bfloat16), "ctx", swap_pairs(2, 1))
    summed = home + got.astype(jnp.float32)
    key_gradient = summed[:, :key_columns]
    value_gradient = summed[:, key_columns:]
    grad_query_raw = (
        reverse_rotation(grad_query, cosine_table, sine_table)
        .astype(jnp.bfloat16)
        .reshape(row_entries, QUERY_HEADS * HEAD_SIZE)
    )
    unrotated_key_gradient = (
        reverse_rotation(
            key_gradient.reshape(row_entries, KEY_VALUE_HEADS, HEAD_SIZE), cosine_table, sine_table
        )
        .astype(jnp.bfloat16)
        .reshape(row_entries, KEY_VALUE_HEADS * HEAD_SIZE)
    )
    plain_value_gradient = value_gradient.astype(jnp.bfloat16)
    grad_w_query = jnp.dot(first_normed.T, grad_query_raw, preferred_element_type=jnp.float32)
    grad_w_key = jnp.dot(first_normed.T, unrotated_key_gradient, preferred_element_type=jnp.float32)
    grad_w_value = jnp.dot(first_normed.T, plain_value_gradient, preferred_element_type=jnp.float32)
    grad_normed_one = jnp.dot(grad_query_raw, w_query.T, preferred_element_type=jnp.float32)
    grad_normed_one = grad_normed_one + jnp.dot(
        unrotated_key_gradient, key_matrix.T, preferred_element_type=jnp.float32
    )
    grad_normed_one = grad_normed_one + jnp.dot(
        plain_value_gradient, value_matrix.T, preferred_element_type=jnp.float32
    )
    grad_input_part, grad_gain_one = norm_back(grad_normed_one, scaled_one, inv_one, gain_one)
    grad_tokens = (grad_hidden + grad_input_part).astype(jnp.bfloat16)
    attn_term = jnp.concatenate(
        [
            grad_w_query.astype(low).reshape(-1, LANES),
            grad_w_key.astype(low).reshape(-1, LANES),
            grad_w_value.astype(low).reshape(-1, LANES),
            grad_w_out.astype(low).reshape(-1, LANES),
            jnp.concatenate([grad_gain_one, grad_gain_two]).astype(low).reshape(-1, LANES),
        ],
        axis=0,
    )
    starts = [owner * attn_columns // (16 * LANES) * 16 for owner in range(owners)]
    ends = [-(-(owner + 1) * attn_columns // LANES) for owner in range(owners)]
    window = max(-(-(end - start) // 32) * 32 for start, end in zip(starts, ends))
    attn_term = jnp.pad(attn_term, ((0, starts[-1] + window - attn_term.shape[0]), (0, 0)))
    attn_table = jnp.stack([attn_term[start : start + window] for start in starts])
    attn_parts = open_parts(attn_table, owners)
    for step in range(steps):
        attn_parts = step_parts(attn_parts, step, owners, shard_index)
    attn_window = close_parts(attn_parts)
    shift = lax.rem(shard_index * attn_columns, 16 * LANES)
    attn_grad = lax.dynamic_slice_in_dim(attn_window, shift, attn_columns, 0)
    attn_new, attn_first_new, attn_second_new = adam_update(
        attn_params, attn_first, attn_second, attn_grad
    )
    ffn_new, ffn_first_new, ffn_second_new = adam_update(
        ffn_params, ffn_first, ffn_second, ffn_joined
    )
    return (
        outputs,
        grad_tokens,
        attn_grad,
        ffn_joined,
        attn_new,
        attn_first_new,
        attn_second_new,
        ffn_new,
        ffn_first_new,
        ffn_second_new,
    )


def solution(mesh):
    return jax.shard_map(
        body,
        mesh=mesh,
        in_specs=(
            P(("shard", "ctx"), None),
            P(("shard", "ctx"), None),
            P("shard"),
            P("shard"),
            P("shard"),
            P("shard"),
            P("shard"),
            P("shard"),
            P("shard"),
        ),
        out_specs=(
            P(("shard", "ctx"), None),
            P(("shard", "ctx"), None),
            P("shard"),
            P("shard"),
            P("shard"),
            P("shard"),
            P("shard"),
            P("shard"),
            P("shard"),
            P("shard"),
        ),
        check_vma=False,
    )
```

```python
import math

import jax
import jax.numpy as jnp
from jax import lax
from jax.sharding import PartitionSpec as P

MODEL_WIDTH = 576
QUERY_HEADS = 9
KEY_VALUE_HEADS = 3
HEAD_SIZE = 64
FF = 1536
ADAM_STEP = 3


rms_eps = 1e-05
rope_base = 100000.0
beta_one = 0.9
beta_two = 0.95
learn_rate = 0.02
decay_rate = 0.1
adam_eps = 1e-08
masked_score = -1e30


def split_flattened(flattened, shapes):
    pieces = []
    offset = 0
    for shape in shapes:
        width = 1
        for extent in shape:
            width = width * extent
        pieces.append(flattened[offset : offset + width].reshape(shape))
        offset = offset + width
    return pieces


def split_attention(flattened):
    return split_flattened(
        flattened,
        (
            (MODEL_WIDTH, QUERY_HEADS * HEAD_SIZE),
            (MODEL_WIDTH, KEY_VALUE_HEADS * HEAD_SIZE),
            (MODEL_WIDTH, KEY_VALUE_HEADS * HEAD_SIZE),
            (QUERY_HEADS * HEAD_SIZE, MODEL_WIDTH),
            (MODEL_WIDTH,),
            (MODEL_WIDTH,),
        ),
    )


def split_feedforward(flattened):
    return split_flattened(flattened, ((MODEL_WIDTH, FF), (MODEL_WIDTH, FF), (FF, MODEL_WIDTH)))


def rope_tables(positions):
    index = jnp.arange(HEAD_SIZE // 2).astype(jnp.float32)
    inverse = jnp.exp(index * (-2.0 * math.log(rope_base) / HEAD_SIZE))
    angles = positions.astype(jnp.float32)[:, None] * inverse[None, :]
    angles = jnp.concatenate([angles, angles], axis=1)
    return (jnp.cos(angles), jnp.sin(angles))


def apply_rotation(values, cosine_table, sine_table):
    half = values.shape[-1] // 2
    turned = jnp.concatenate([-values[..., half:], values[..., :half]], axis=-1)
    return values * cosine_table[:, None, :] + turned * sine_table[:, None, :]


def reverse_rotation(grads, cosine_table, sine_table):
    half = grads.shape[-1] // 2
    weighted = grads * sine_table[:, None, :]
    turned = jnp.concatenate([weighted[..., half:], -weighted[..., :half]], axis=-1)
    return grads * cosine_table[:, None, :] + turned


def norm_rows(values, gain):
    mean_sq = jnp.mean(values * values, axis=-1, keepdims=True)
    inverse = lax.rsqrt(mean_sq + rms_eps)
    scaled = values * inverse
    return (scaled, inverse, (scaled * gain).astype(jnp.bfloat16))


def norm_back(grad_normed, scaled, inverse, gain):
    grad_scaled = grad_normed * gain
    grad_gain = jnp.sum(grad_normed * scaled, axis=0)
    inner = jnp.mean(grad_scaled * scaled, axis=-1, keepdims=True)
    return (inverse * (grad_scaled - scaled * inner), grad_gain)


def attend(query_rows, keys, values, mask):
    row_entries = query_rows.shape[0]
    scale = 1.0 / math.sqrt(HEAD_SIZE)
    grouped_heads = query_rows.reshape(
        row_entries, KEY_VALUE_HEADS, QUERY_HEADS // KEY_VALUE_HEADS, HEAD_SIZE
    )
    scores = (
        jnp.einsum("tkgd,skd->kgts", grouped_heads, keys, preferred_element_type=jnp.float32)
        * scale
    )
    scores = jnp.where(mask[None, None], scores, masked_score)
    top = jnp.max(scores, axis=-1, keepdims=True)
    total = jnp.sum(jnp.exp(scores - top), axis=-1, keepdims=True)
    log_total = top + jnp.log(total)
    probs = jnp.exp(scores - log_total).astype(jnp.bfloat16)
    mixture = jnp.einsum("kgts,skd->tkgd", probs, values, preferred_element_type=jnp.float32)
    return (mixture.reshape(row_entries, QUERY_HEADS * HEAD_SIZE).astype(jnp.bfloat16), log_total)


def attend_back(
    query_rows, keys, values, mask, log_total, mixture, mixture_gradient
):
    row_entries = query_rows.shape[0]
    head_group = QUERY_HEADS // KEY_VALUE_HEADS
    scale = 1.0 / math.sqrt(HEAD_SIZE)
    grouped_queries = query_rows.reshape(
        row_entries, KEY_VALUE_HEADS, head_group, HEAD_SIZE
    ).transpose(1, 0, 2, 3)
    gradient_groups = mixture_gradient.reshape(
        row_entries, KEY_VALUE_HEADS, head_group, HEAD_SIZE
    ).transpose(1, 0, 2, 3)
    mixture_groups = mixture.reshape(row_entries, KEY_VALUE_HEADS, head_group, HEAD_SIZE).transpose(
        1, 0, 2, 3
    )
    key_groups = keys.transpose(1, 0, 2)
    value_groups = values.transpose(1, 0, 2)

    def one_group(item):
        query_one, key_one, value_one, total_one, mixed_one, grad_one = item
        scores = (
            jnp.einsum("tgd,sd->gts", query_one, key_one, preferred_element_type=jnp.float32)
            * scale
        )
        scores = jnp.where(mask[None], scores, masked_score)
        probs = jnp.exp(scores - total_one)
        delta = jnp.einsum("tgd,tgd->gt", grad_one, mixed_one, preferred_element_type=jnp.float32)
        grad_probs = jnp.einsum(
            "tgd,sd->gts", grad_one, value_one, preferred_element_type=jnp.float32
        )
        grad_scores = (probs * (grad_probs - delta[..., None]) * scale).astype(jnp.bfloat16)
        grad_query = jnp.einsum(
            "gts,sd->tgd", grad_scores, key_one, preferred_element_type=jnp.float32
        )
        key_gradient = jnp.einsum(
            "gts,tgd->sd", grad_scores, query_one, preferred_element_type=jnp.float32
        )
        value_gradient = jnp.einsum(
            "gts,tgd->sd", probs.astype(jnp.bfloat16), grad_one, preferred_element_type=jnp.float32
        )
        return (grad_query, key_gradient, value_gradient)

    results = [
        one_group(
            (
                grouped_queries[group],
                key_groups[group],
                value_groups[group],
                log_total[group],
                mixture_groups[group],
                gradient_groups[group],
            )
        )
        for group in range(KEY_VALUE_HEADS)
    ]
    grad_query, key_gradient, value_gradient = [jnp.stack(item) for item in zip(*results)]
    grad_query = grad_query.transpose(1, 0, 2, 3).reshape(row_entries, QUERY_HEADS, HEAD_SIZE)
    return (grad_query, key_gradient.transpose(1, 0, 2), value_gradient.transpose(1, 0, 2))


def adam_update(params, first, second, grads):
    first_new = beta_one * first + (1.0 - beta_one) * grads
    second_new = beta_two * second + (1.0 - beta_two) * grads * grads
    corr_one = 1.0 - beta_one**ADAM_STEP
    corr_two = 1.0 - beta_two**ADAM_STEP
    moved = first_new / corr_one / (jnp.sqrt(second_new / corr_two) + adam_eps)
    return (params - learn_rate * (moved + decay_rate * params), first_new, second_new)


LANES = 128


def swap_pairs(count, distance):
    return [(index, index ^ distance) for index in range(count)]


CTX = -1


def halve_stage(table, bits, bit, owners, index):
    if bit == CTX:
        axis, mine = table.ndim - 2, lax.axis_index("ctx")
        shape = table.shape
        table = table.reshape(shape[:axis] + (2, shape[axis] // 2, LANES))
    else:
        axis, mine = bits.index(bit), (index >> bit) & 1
    send = lax.dynamic_index_in_dim(table, 1 - mine, axis, keepdims=False)
    keep = lax.dynamic_index_in_dim(table, mine, axis, keepdims=False)
    if bit == CTX:
        got = lax.ppermute(send, "ctx", swap_pairs(2, 1))
    else:
        got = lax.ppermute(send, "shard", swap_pairs(owners, 1 << bit))
    total = keep.astype(jnp.float32) + got.astype(jnp.float32)
    bits = [b for b in bits if b != bit]
    if bits:
        total = total.astype(jnp.bfloat16)
    return total, bits


def bit_orders(owners):
    low = list(range(owners.bit_length() - 1))
    return (low, [0, CTX] + low[1:])


def open_parts(table, owners):
    count = owners.bit_length() - 1
    rows = table.shape[1]
    cut = rows - rows // 64 * 32
    pieces = (table[:, :cut], table[:, cut:])
    return [
        (piece.reshape((2,) * count + piece.shape[1:]), list(range(count))[::-1])
        for piece in pieces
    ]


def step_parts(parts, step, owners, index):
    return [
        halve_stage(table, bits, order[step], owners, index) if step < len(order) else (table, bits)
        for (table, bits), order in zip(parts, bit_orders(owners))
    ]


def tie(parts, other):
    tables, other = lax.optimization_barrier(([table for table, _ in parts], other))
    return [(table, bits) for table, (_, bits) in zip(tables, parts)], other


def close_parts(parts):
    (one, _), (two, _) = parts
    one = one.astype(jnp.bfloat16)
    one_got = lax.ppermute(one, "ctx", swap_pairs(2, 1))
    two_got = lax.ppermute(two, "ctx", swap_pairs(2, 1))
    first = lax.axis_index("ctx") == 0
    return jnp.concatenate(
        [
            one.astype(jnp.float32) + one_got.astype(jnp.float32),
            jnp.where(first, two, two_got),
            jnp.where(first, two_got, two),
        ],
        axis=0,
    ).reshape(-1)


def doubling_gather(share, owners, index):
    count = owners.bit_length() - 1
    table = share
    for place, bit in enumerate(range(count)[::-1]):
        got = lax.ppermute(table, "shard", swap_pairs(owners, 1 << bit))
        low_first = ((index >> bit) & 1) == 0
        table = jnp.stack(
            [jnp.where(low_first, table, got), jnp.where(low_first, got, table)], axis=place
        )
    return table.reshape((owners,) + share.shape)


def body(
    tokens,
    cotangent,
    seq_lengths,
    attn_params,
    attn_first,
    attn_second,
    ffn_params,
    ffn_first,
    ffn_second,
):
    row_entries = tokens.shape[0]
    ctx_count = lax.axis_size("ctx")
    ctx_index = lax.axis_index("ctx")
    owners = lax.axis_size("shard")
    slot_entries = row_entries * ctx_count
    length = seq_lengths[0]
    attn_columns = attn_params.shape[0]
    attn_rows = -(-attn_columns // (16 * LANES)) * 16
    attn_pad = attn_rows * LANES - attn_columns
    attn_low = jnp.pad(attn_params.astype(jnp.bfloat16), (0, attn_pad))
    shard_index = lax.axis_index("shard")
    attn_whole = doubling_gather(attn_low.reshape(attn_rows, LANES), owners, shard_index)
    attn_whole = attn_whole.reshape(owners, attn_rows * LANES)[:, :attn_columns].reshape(-1)
    ffn_whole = lax.all_gather(ffn_params.astype(jnp.bfloat16), "shard", axis=0, tiled=True)
    w_query, key_matrix, value_matrix, w_out, gain_one, gain_two = split_attention(attn_whole)
    w_gate, w_up, w_down = split_feedforward(ffn_whole)
    gain_one = gain_one.astype(jnp.float32)
    gain_two = gain_two.astype(jnp.float32)
    positions = ctx_index * row_entries + jnp.arange(row_entries)
    key_positions = jnp.arange(slot_entries)
    valid = (positions < length).astype(jnp.float32)[:, None]
    mask = (key_positions[None, :] <= positions[:, None]) & (key_positions[None, :] < length)
    inputs = tokens.astype(jnp.float32)
    scaled_one, inv_one, first_normed = norm_rows(inputs, gain_one)
    query_raw = jnp.dot(first_normed, w_query, preferred_element_type=jnp.float32).reshape(
        row_entries, QUERY_HEADS, HEAD_SIZE
    )
    unrotated_key = jnp.dot(first_normed, key_matrix, preferred_element_type=jnp.float32).reshape(
        row_entries, KEY_VALUE_HEADS, HEAD_SIZE
    )
    value_reduced = jnp.dot(first_normed, value_matrix, preferred_element_type=jnp.float32).astype(
        jnp.bfloat16
    )
    cosine_table, sine_table = rope_tables(positions)
    query_low = apply_rotation(query_raw, cosine_table, sine_table).astype(jnp.bfloat16)
    key_reduced = (
        apply_rotation(unrotated_key, cosine_table, sine_table)
        .astype(jnp.bfloat16)
        .reshape(row_entries, KEY_VALUE_HEADS * HEAD_SIZE)
    )
    key_columns = KEY_VALUE_HEADS * HEAD_SIZE
    both = jnp.concatenate([key_reduced, value_reduced], axis=1)
    other_both = lax.ppermute(both, "ctx", swap_pairs(2, 1))
    first = ctx_index == 0
    full_both = jnp.concatenate(
        [jnp.where(first, both, other_both), jnp.where(first, other_both, both)], axis=0
    )
    full_keys = full_both[:, :key_columns]
    full_values = full_both[:, key_columns:]
    full_keys = full_keys.reshape(slot_entries, KEY_VALUE_HEADS, HEAD_SIZE)
    full_values = full_values.reshape(slot_entries, KEY_VALUE_HEADS, HEAD_SIZE)
    mixture, log_total = attend(query_low, full_keys, full_values, mask)
    hidden = inputs + jnp.dot(mixture, w_out, preferred_element_type=jnp.float32)
    scaled_two, inv_two, normed_two = norm_rows(hidden, gain_two)
    gate = jnp.dot(normed_two, w_gate, preferred_element_type=jnp.float32)
    upward = jnp.dot(normed_two, w_up, preferred_element_type=jnp.float32)
    sigma = jax.nn.sigmoid(gate)
    activ = (gate * sigma * upward).astype(jnp.bfloat16)
    result = hidden + jnp.dot(activ, w_down, preferred_element_type=jnp.float32)
    outputs = (valid * result).astype(jnp.bfloat16)
    grad_result = valid * cotangent.astype(jnp.float32)
    grad_low = grad_result.astype(jnp.bfloat16)
    grad_w_down = jnp.dot(activ.T, grad_low, preferred_element_type=jnp.float32)
    grad_activ = jnp.dot(grad_low, w_down.T, preferred_element_type=jnp.float32)
    grad_gate = (grad_activ * upward * sigma * (1.0 + gate * (1.0 - sigma))).astype(jnp.bfloat16)
    grad_upward = (grad_activ * gate * sigma).astype(jnp.bfloat16)
    grad_w_gate = jnp.dot(normed_two.T, grad_gate, preferred_element_type=jnp.float32)
    grad_w_up = jnp.dot(normed_two.T, grad_upward, preferred_element_type=jnp.float32)
    low = jnp.bfloat16
    ffn_term = jnp.concatenate(
        [
            grad_w_gate.astype(low).reshape(-1),
            grad_w_up.astype(low).reshape(-1),
            grad_w_down.astype(low).reshape(-1),
        ]
    )
    ffn_parts = open_parts(ffn_term.reshape(owners, -1, LANES), owners)
    grad_normed_two = jnp.dot(grad_gate, w_gate.T, preferred_element_type=jnp.float32) + jnp.dot(
        grad_upward, w_up.T, preferred_element_type=jnp.float32
    )
    grad_hidden_part, grad_gain_two = norm_back(grad_normed_two, scaled_two, inv_two, gain_two)
    grad_hidden = grad_result + grad_hidden_part
    grad_hidden_low = grad_hidden.astype(jnp.bfloat16)
    grad_w_out = jnp.dot(mixture.T, grad_hidden_low, preferred_element_type=jnp.float32)
    mixture_gradient = jnp.dot(grad_hidden_low, w_out.T, preferred_element_type=jnp.float32).astype(
        jnp.bfloat16
    )
    steps = owners.bit_length()
    ffn_parts = step_parts(ffn_parts, 0, owners, shard_index)
    ffn_parts, mixture_gradient = tie(ffn_parts, mixture_gradient)
    grad_query, full_key_gradient, full_value_gradient = attend_back(
        query_low, full_keys, full_values, mask, log_total, mixture, mixture_gradient
    )
    ffn_parts = step_parts(ffn_parts, 1, owners, shard_index)
    ffn_parts, (full_key_gradient, full_value_gradient) = tie(
        ffn_parts, (full_key_gradient, full_value_gradient)
    )
    full_gradient = jnp.concatenate(
        [
            full_key_gradient.reshape(slot_entries, key_columns),
            full_value_gradient.reshape(slot_entries, key_columns),
        ],
        axis=1,
    )
    halves = full_gradient.reshape(2, row_entries, 2 * key_columns)
    away = lax.dynamic_index_in_dim(halves, 1 - ctx_index, 0, keepdims=False)
    home = lax.dynamic_index_in_dim(halves, ctx_index, 0, keepdims=False)
    got = lax.ppermute(away.astype(jnp.bfloat16), "ctx", swap_pairs(2, 1))
    ffn_parts = step_parts(ffn_parts, 2, owners, shard_index)
    ffn_parts, got = tie(ffn_parts, got)
    summed = home + got.astype(jnp.float32)
    key_gradient = summed[:, :key_columns]
    value_gradient = summed[:, key_columns:]
    grad_query_raw = (
        reverse_rotation(grad_query, cosine_table, sine_table)
        .astype(jnp.bfloat16)
        .reshape(row_entries, QUERY_HEADS * HEAD_SIZE)
    )
    unrotated_key_gradient = (
        reverse_rotation(
            key_gradient.reshape(row_entries, KEY_VALUE_HEADS, HEAD_SIZE), cosine_table, sine_table
        )
        .astype(jnp.bfloat16)
        .reshape(row_entries, KEY_VALUE_HEADS * HEAD_SIZE)
    )
    plain_value_gradient = value_gradient.astype(jnp.bfloat16)
    grad_w_query = jnp.dot(first_normed.T, grad_query_raw, preferred_element_type=jnp.float32)
    grad_w_key = jnp.dot(first_normed.T, unrotated_key_gradient, preferred_element_type=jnp.float32)
    grad_w_value = jnp.dot(first_normed.T, plain_value_gradient, preferred_element_type=jnp.float32)
    grad_normed_one = jnp.dot(grad_query_raw, w_query.T, preferred_element_type=jnp.float32)
    grad_normed_one = grad_normed_one + jnp.dot(
        unrotated_key_gradient, key_matrix.T, preferred_element_type=jnp.float32
    )
    grad_normed_one = grad_normed_one + jnp.dot(
        plain_value_gradient, value_matrix.T, preferred_element_type=jnp.float32
    )
    ffn_parts = step_parts(ffn_parts, 3, owners, shard_index)
    ffn_parts, grad_normed_one = tie(ffn_parts, grad_normed_one)
    grad_input_part, grad_gain_one = norm_back(grad_normed_one, scaled_one, inv_one, gain_one)
    grad_tokens = (grad_hidden + grad_input_part).astype(jnp.bfloat16)
    for step in range(4, steps):
        ffn_parts = step_parts(ffn_parts, step, owners, shard_index)
    ffn_joined = close_parts(ffn_parts)
    attn_term = jnp.concatenate(
        [
            grad_w_query.astype(low).reshape(-1, LANES),
            grad_w_key.astype(low).reshape(-1, LANES),
            grad_w_value.astype(low).reshape(-1, LANES),
            grad_w_out.astype(low).reshape(-1, LANES),
            jnp.concatenate([grad_gain_one, grad_gain_two]).astype(low).reshape(-1, LANES),
        ],
        axis=0,
    )
    starts = [owner * attn_columns // (16 * LANES) * 16 for owner in range(owners)]
    ends = [-(-(owner + 1) * attn_columns // LANES) for owner in range(owners)]
    window = max(-(-(end - start) // 32) * 32 for start, end in zip(starts, ends))
    attn_term = jnp.pad(attn_term, ((0, starts[-1] + window - attn_term.shape[0]), (0, 0)))
    attn_table = jnp.stack([attn_term[start : start + window] for start in starts])
    attn_parts = open_parts(attn_table, owners)
    for step in range(steps):
        attn_parts = step_parts(attn_parts, step, owners, shard_index)
    attn_window = close_parts(attn_parts)
    shift = lax.rem(shard_index * attn_columns, 16 * LANES)
    attn_grad = lax.dynamic_slice_in_dim(attn_window, shift, attn_columns, 0)
    attn_new, attn_first_new, attn_second_new = adam_update(
        attn_params, attn_first, attn_second, attn_grad
    )
    ffn_new, ffn_first_new, ffn_second_new = adam_update(
        ffn_params, ffn_first, ffn_second, ffn_joined
    )
    return (
        outputs,
        grad_tokens,
        attn_grad,
        ffn_joined,
        attn_new,
        attn_first_new,
        attn_second_new,
        ffn_new,
        ffn_first_new,
        ffn_second_new,
    )


def solution(mesh):
    return jax.shard_map(
        body,
        mesh=mesh,
        in_specs=(
            P(("shard", "ctx"), None),
            P(("shard", "ctx"), None),
            P("shard"),
            P("shard"),
            P("shard"),
            P("shard"),
            P("shard"),
            P("shard"),
            P("shard"),
        ),
        out_specs=(
            P(("shard", "ctx"), None),
            P(("shard", "ctx"), None),
            P("shard"),
            P("shard"),
            P("shard"),
            P("shard"),
            P("shard"),
            P("shard"),
            P("shard"),
            P("shard"),
        ),
        check_vma=False,
    )
```
